32 devices in a mesh: tm: 4 (over z), row: 8 (over y, x, core).
Axes of the slice: x: 2, y: 2, z: 4, core: 2. Of those that a mesh axis runs over, the one named last changes fastest.
Arguments:
- features: bfloat16 [256, 8, 37, 256], P('row', 'tm'), may hold values from -8 to 8
- frame_mask: int32 [256], P('row'), may hold values from 0 to 1, as said below
- norm_gain: float32 [256], replicated, may hold values from 0.25 to 1.75
- input_weight: bfloat16 [256, 768], replicated, may hold values from -12 to 12
- output_weight: bfloat16 [256, 256], replicated, may hold values from -0.375 to 0.375
- first_kernel: bfloat16 [9, 256, 128], replicated, may hold values from -0.125 to 0.125
- first_bias: float32 [128], replicated, may hold values from -3 to 3
- second_kernel: bfloat16 [9, 128, 32], replicated, may hold values from -0.1875 to 0.1875
- second_bias: float32 [32], replicated, may hold values from -3 to 3
Outputs:
- depth_head: bfloat16 [256, 8, 1184], P('row', 'tm')
The draws below stay inside these ranges and needn't reach their ends.
Inputs may be any that keep to these rules, and one draw needn't show every extreme that they name: frame_mask is 1 on frames 0 to n - 1 and 0 on the rest, for some n with 192 < n < 256.
All inputs are finite; a program needn't handle non-finite values.
Results may differ from the reference program's by a relative error of at most 0.0057.
Values may be sent and summed in bfloat16 or wider, within the bound.
A program may use at most 128 MiB of HBM per device.

```python
import math
import jax
import jax.numpy as jnp
from jax import lax

C = 256
HEADS = 8
C1 = 128
C2 = 32
WIN = 32
W = 37
F_DEV = 32
FRAMES = 256
H = 8


def draw_features(key, part):
    base = jax.random.normal(key, (FRAMES, H, W, C), jnp.float32)
    return jnp.clip(base, -6.0, 6.0).astype(jnp.bfloat16)


def draw_frame_mask(key, part):
    count = jax.random.randint(key, (), FRAMES - 2 * F_DEV + 1, FRAMES)
    return (jnp.arange(FRAMES) < count).astype(jnp.int32)


def draw_input_weight(key, part):
    raw = jnp.clip(jax.random.normal(key, (C, 3 * C), jnp.float32), -4.0, 4.0) * C ** (-0.5)
    return raw.astype(jnp.bfloat16)


def normal_values(rng, extent, deviation, most, kind=jnp.bfloat16):
    array = jax.random.normal(rng, extent, jnp.float32) * deviation
    return jnp.minimum(jnp.maximum(array, -most), most).astype(kind)


def setup_inputs(seed: int = 0) -> dict:
    streams_of = jax.random.split(jax.random.key(seed), 10)
    features = draw_features(jax.random.fold_in(streams_of[9], 71), 0)
    frame_mask = draw_frame_mask(jax.random.fold_in(streams_of[9], 71), 0)
    norm_gain = jnp.clip(1.0 + 0.15 * jax.random.normal(streams_of[2], (C,), jnp.float32), 0.25, 1.75)
    input_weight = draw_input_weight(jax.random.fold_in(streams_of[9], 71), 0)
    output_weight = normal_values(streams_of[4], (C, C), C ** -0.5, 0.375)
    first_kernel = normal_values(streams_of[5], (9, C, C1), (9 * C) ** -0.5, 0.125)
    first_bias = normal_values(streams_of[6], (C1,), 0.5, 3.0, jnp.float32)
    second_kernel = normal_values(streams_of[7], (9, C1, C2), (9 * C1) ** -0.5, 0.1875)
    second_bias = normal_values(streams_of[8], (C2,), 0.5, 3.0, jnp.float32)
    return {"features": features, "frame_mask": frame_mask, "norm_gain": norm_gain, "input_weight": input_weight, "output_weight": output_weight, "first_kernel": first_kernel, "first_bias": first_bias, "second_kernel": second_kernel, "second_bias": second_bias}


epsilon = 1e-05

def layer_norm(field, norm_gain):
    widened = field.astype(jnp.float32)
    average = lax.optimization_barrier(jnp.mean(widened, axis=-1, keepdims=True))
    centered = widened - average
    variance = lax.optimization_barrier(jnp.mean(centered * centered, axis=-1, keepdims=True))
    return (centered * lax.rsqrt(variance + epsilon) * norm_gain).astype(jnp.bfloat16)

def convolve(field, kernel, bias):
    padded = jnp.pad(field, ((0, 0), (1, 1), (1, 1), (0, 0)))
    height = field.shape[1]
    width = field.shape[2]
    running = jnp.zeros(field.shape[:3] + (kernel.shape[2],), jnp.float32)
    for tap_row in range(3):
        for tap_col in range(3):
            window = padded[:, tap_row:tap_row + height, tap_col:tap_col + width].astype(jnp.float32)
            running = running + jnp.einsum('frwc,cd->frwd', window, kernel[3 * tap_row + tap_col].astype(jnp.float32))
    return jnp.maximum(running + bias, 0.0)

def reference(features, frame_mask, norm_gain, input_weight, output_weight, first_kernel, first_bias, second_kernel, second_bias):
    frames, height, width, channels = features.shape
    places = height * width
    head_size = channels // HEADS
    block_count = frames // WIN
    out_width = second_kernel.shape[2]

    def one_block(block_id):
        first_frame = block_id * WIN
        earlier_start = jnp.maximum(first_frame - WIN, 0).astype(jnp.int32)
        current = lax.dynamic_slice_in_dim(features, first_frame, WIN, 0)
        earlier = lax.dynamic_slice_in_dim(features, earlier_start, WIN, 0)
        current_mask = lax.dynamic_slice_in_dim(frame_mask, first_frame, WIN, 0)
        earlier_mask = lax.dynamic_slice_in_dim(frame_mask, earlier_start, WIN, 0) * (block_id > 0).astype(jnp.int32)
        window_frames = jnp.concatenate([earlier, current], axis=0).reshape(2 * WIN, places, channels)
        normed = layer_norm(window_frames, norm_gain)
        projected = jnp.einsum('fpc,cd->fpd', normed.astype(jnp.float32), input_weight.astype(jnp.float32)).astype(jnp.bfloat16)
        query_part = projected[WIN:, :, :channels].reshape(WIN, places, HEADS, head_size).astype(jnp.float32)
        key_part = projected[:, :, channels:2 * channels].reshape(2 * WIN, places, HEADS, head_size).astype(jnp.float32)
        value_part = projected[:, :, 2 * channels:].reshape(2 * WIN, places, HEADS, head_size).astype(jnp.float32)
        scores = jnp.einsum('iphd,jphd->phij', query_part, key_part) * (1.0 / math.sqrt(head_size))
        mask_pairs = jnp.concatenate([earlier_mask, current_mask])
        query_pos = jnp.arange(WIN, dtype=jnp.int32)[:, None]
        key_pos = jnp.arange(2 * WIN, dtype=jnp.int32)[None, :]
        inside = (key_pos >= query_pos + 1) & (key_pos <= query_pos + WIN)
        itself = key_pos == query_pos + WIN
        allowed = inside & ((mask_pairs[None, :] == 1) | itself)
        scores = jnp.where(allowed[None, None], scores, -1e+30)
        largest = lax.optimization_barrier(jnp.max(scores, axis=-1, keepdims=True))
        powers = jnp.exp(scores - largest)
        weights = (powers / lax.optimization_barrier(jnp.sum(powers, axis=-1, keepdims=True))).astype(jnp.bfloat16)
        attended = jnp.einsum('phij,jphd->iphd', weights.astype(jnp.float32), value_part).astype(jnp.bfloat16)
        attended = attended.reshape(WIN, places, channels)
        branch = jnp.einsum('fpc,cd->fpd', attended.astype(jnp.float32), output_weight.astype(jnp.float32))
        mixed = (current.reshape(WIN, places, channels).astype(jnp.float32) + branch).astype(jnp.bfloat16)
        mixed = mixed.reshape(WIN, height, width, channels)
        hidden = convolve(mixed, first_kernel, first_bias).astype(jnp.bfloat16)
        outcome = convolve(hidden, second_kernel, second_bias).astype(jnp.bfloat16)
        return outcome.reshape(WIN, height, width * out_width)
    result = lax.map(one_block, jnp.arange(block_count, dtype=jnp.int32))
    return result.reshape(frames, height, width * out_width)
```

```python
import functools
import math

import jax
import jax.numpy as jnp
from jax import lax
from jax.experimental import pallas as pl
from jax.experimental.pallas import tpu as pltpu
from jax.sharding import PartitionSpec as P

HEADS = 8
WIN = 32
TAPS = 3
GROUP = 4
NEG = -1e30
epsilon = 1e-05
MESH = pl.DeviceIdType.MESH
F32 = jnp.float32
BF16 = jnp.bfloat16


def layer_norm(field, gain):
    widened = field.astype(F32)
    average = jnp.mean(widened, axis=-1, keepdims=True)
    centered = widened - average
    variance = jnp.mean(centered * centered, axis=-1, keepdims=True)
    return (centered * lax.rsqrt(variance + epsilon) * gain).astype(BF16)


def dot(a, b):
    return jnp.dot(a, b, preferred_element_type=F32)


def dot_t(a, b):
    return lax.dot_general(a, b, (((1,), (1,)), ((), ())), preferred_element_type=F32)


def dot_tt(a, b):
    return lax.dot_general(a, b, (((0,), (0,)), ((), ())), preferred_element_type=F32)


def kernel(
    width,
    bounds,
    n_row,
    n_tm,
    x_ref,
    mask_ref,
    gain_ref,
    win_ref,
    wout_ref,
    k1_ref,
    b1_ref,
    k2_ref,
    b2_ref,
    o_ref,
    halo,
    pmask,
    qkv,
    hkv,
    att,
    headmask,
    bias,
    grid_x,
    w1,
    w2,
    acc,
    p_up,
    p_down,
    r_up,
    r_down,
    hid,
    acc2,
    s_up,
    s_down,
    t_up,
    t_down,
    send_sem,
    recv_sem,
):
    frames = WIN
    channels = x_ref.shape[1]
    head_size = channels // HEADS
    half = HEADS // 2
    tokens = width * frames
    c1 = k1_ref.shape[2]
    c2 = k2_ref.shape[1]
    row = lax.axis_index("row")
    tm = lax.axis_index("tm")
    has_prev, has_next = row > 0, row < n_row - 1
    has_up, has_down = tm > 0, tm < n_tm - 1

    barrier = pltpu.get_barrier_semaphore()
    sides = (
        (has_prev, {"row": row - 1}),
        (has_next, {"row": row + 1}),
        (has_up, {"tm": tm - 1}),
        (has_down, {"tm": tm + 1}),
    )
    for present, where in sides:

        @pl.when(present)
        def _(where=where):
            pl.semaphore_signal(barrier, inc=1, device_id=where, device_id_type=MESH)

    pl.semaphore_wait(barrier, sum(present.astype(jnp.int32) for present, _ in sides))

    def copy(src, dst, slot, where):
        return pltpu.make_async_remote_copy(
            src_ref=src,
            dst_ref=dst,
            send_sem=send_sem.at[slot],
            recv_sem=recv_sem.at[slot],
            device_id=where,
            device_id_type=MESH,
        )

    nxt = {"row": row + 1}
    chunks = len(bounds) - 1
    halo_copies = [copy(mask_ref, pmask, chunks, nxt)]
    for c in range(chunks):
        part = pl.ds(bounds[c] * frames, (bounds[c + 1] - bounds[c]) * frames)
        halo_copies.append(copy(x_ref.at[part], halo.at[part], c, nxt))

    @pl.when(has_next)
    def _():
        for one in halo_copies:
            one.start()

    @pl.when(jnp.logical_not(has_prev))
    def _():
        halo[...] = jnp.zeros_like(halo)
        pmask[...] = jnp.zeros_like(pmask)

    up, down = {"tm": tm - 1}, {"tm": tm + 1}
    first_up = copy(p_up, r_down, chunks + 1, up)
    first_down = copy(p_down, r_up, chunks + 2, down)
    second_up = copy(s_up, t_down, chunks + 3, up)
    second_down = copy(s_down, t_up, chunks + 4, down)

    for tap in range(TAPS * TAPS):
        a, b = tap // TAPS, tap % TAPS
        w1[b * channels : (b + 1) * channels, a * c1 : (a + 1) * c1] = k1_ref[tap]
    w2[...] = jnp.zeros_like(w2)
    for a in range(TAPS):
        for o in range(GROUP):
            for b in range(TAPS):
                r0 = (a * GROUP + o) * c2
                w2[r0 : r0 + c2, (o + b) * c1 : (o + b + 1) * c1] = k2_ref[a * TAPS + b]
    for r in range(2):
        grid_x[r, 0:frames] = jnp.zeros((frames, channels), BF16)
        grid_x[r, tokens + frames : tokens + 2 * frames] = jnp.zeros((frames, channels), BF16)
        hid[r] = jnp.zeros_like(hid[r])

    lane = lax.broadcasted_iota(jnp.int32, (HEADS * frames, channels), 1)
    sub = lax.broadcasted_iota(jnp.int32, (HEADS * frames, channels), 0)
    headmask[...] = (lane // head_size == sub // frames).astype(F32).astype(BF16)

    gain = gain_ref[...]
    total = 2 * tokens
    block = total // 4

    def project(i, carry):
        at = pl.multiple_of(i * block, 16)
        normed = layer_norm(x_ref[pl.ds(at, block)], gain)
        qkv[pl.ds(at, block)] = dot(normed, win_ref[...]).astype(BF16)
        return carry

    lax.fori_loop(0, 4, project, 0)

    scale = 1.0 / math.sqrt(head_size)
    slot_s = lax.broadcasted_iota(jnp.int32, (frames, HEADS * frames), 0)
    slot_t = lax.broadcasted_iota(jnp.int32, (frames, HEADS * frames), 1) % frames
    own = slot_s <= slot_t

    @pl.when(has_prev)
    def _():
        halo_copies[0].wait_recv()

    m_own = jnp.concatenate([mask_ref[...]] * (HEADS * frames // 128), axis=1)
    m_prev = jnp.concatenate([pmask[...]] * (HEADS * frames // 128), axis=1)
    seen = jnp.where(own, jnp.where(slot_s == slot_t, 1.0, m_own), m_prev)
    bias[...] = jnp.where(seen == 1.0, 0.0, NEG)

    lane_head = lax.broadcasted_iota(jnp.int32, (frames, channels // 2), 1) // head_size

    def place(p):
        rows = pl.ds(pl.multiple_of(p * frames, frames), frames)
        q = qkv[rows, 0:channels]
        k = jnp.concatenate([hkv[rows, 0:channels], qkv[rows, channels : 2 * channels]], axis=0)
        v = jnp.concatenate(
            [hkv[rows, channels : 2 * channels], qkv[rows, 2 * channels : 3 * channels]], axis=0
        )
        spread = jnp.concatenate([q] * HEADS, axis=0) * headmask[...]
        s = dot_t(k, spread)
        s = jnp.where(own, s[frames:], s[:frames]) + bias[...]
        peak = jnp.max(s, axis=0, keepdims=True)
        powers = jnp.exp((s - peak) * scale)
        w = powers * (1.0 / jnp.sum(powers, axis=0, keepdims=True))
        w = jnp.concatenate([jnp.where(own, 0.0, w), jnp.where(own, w, 0.0)], axis=0).astype(BF16)
        outs = []
        for g in range(2):
            cols = slice(g * channels // 2, (g + 1) * channels // 2)
            r = dot_tt(w[:, g * half * frames : (g + 1) * half * frames], v[:, cols])
            total_g = r[0:frames]
            for h in range(1, half):
                total_g = jnp.where(lane_head == h, r[h * frames : (h + 1) * frames], total_g)
            outs.append(total_g)
        att[rows] = jnp.concatenate(outs, axis=1).astype(BF16)

    def pair(i, carry):
        place(2 * i)
        place(2 * i + 1)
        return carry

    tile = tokens // 2

    def finish(r):
        for i in range(2):
            rows = slice(r * tokens + i * tile, r * tokens + (i + 1) * tile)
            mixed = x_ref[rows].astype(F32) + dot(att[rows], wout_ref[...])
            grid_x[r, frames + i * tile : frames + (i + 1) * tile] = mixed.astype(BF16)
        for i in range(2):
            window = jnp.concatenate(
                [grid_x[r, b * frames + i * tile : b * frames + (i + 1) * tile] for b in range(TAPS)],
                axis=1,
            )
            full = dot(window, w1[...])
            rows = slice(i * tile, (i + 1) * tile)
            below, here, above = full[:, 0:c1], full[:, c1 : 2 * c1], full[:, 2 * c1 : 3 * c1]
            if r == 0:
                p_up[rows] = above.astype(BF16)
                acc[0, rows] = here
                acc[1, rows] = below
            else:
                p_down[rows] = below.astype(BF16)
                acc[1, rows] = acc[1, rows] + here
                acc[0, rows] = acc[0, rows] + above

    for c in range(chunks):

        @pl.when(has_prev)
        def _(c=c):
            halo_copies[c + 1].wait_recv()

        part = slice(bounds[c] * frames, bounds[c + 1] * frames)
        normed = layer_norm(halo[part], gain)
        hkv[part] = dot(normed, win_ref[:, channels : 3 * channels]).astype(BF16)
        lax.fori_loop(bounds[c] // 2, bounds[c + 1] // 2, pair, 0)
        if bounds[c] < width <= bounds[c + 1]:
            finish(0)

            @pl.when(has_up)
            def _():
                first_up.start()

    finish(1)

    @pl.when(has_down)
    def _():
        first_down.start()

    @pl.when(jnp.logical_not(has_up))
    def _():
        r_up[...] = jnp.zeros_like(r_up)
        t_up[...] = jnp.zeros_like(t_up)

    @pl.when(jnp.logical_not(has_down))
    def _():
        r_down[...] = jnp.zeros_like(r_down)
        t_down[...] = jnp.zeros_like(t_down)

    b2 = jnp.concatenate([b2_ref[...]] * GROUP, axis=1)
    groups = (width + GROUP - 1) // GROUP
    span = (GROUP + TAPS - 1) * c1

    def hidden_row(r, received):
        for col in range(width):
            rows = slice(col * frames, (col + 1) * frames)
            h = jnp.maximum(acc[r, rows] + received[rows].astype(F32) + b1_ref[...], 0.0)
            hid[r, :, (col + 1) * c1 : (col + 2) * c1] = h.astype(BF16)
        window = jnp.concatenate(
            [hid[r, :, g * GROUP * c1 : g * GROUP * c1 + span] for g in range(groups)], axis=0
        )
        full = dot_t(window, w2[...])
        n = GROUP * c2
        return full[:, 0:n], full[:, n : 2 * n], full[:, 2 * n : 3 * n]

    @pl.when(has_down)
    def _():
        first_up.wait_recv()

    below, here, above = hidden_row(1, r_down)
    s_down[...] = below.astype(BF16)
    acc2[1] = here
    acc2[0] = above

    @pl.when(has_down)
    def _():
        second_down.start()

    @pl.when(has_up)
    def _():
        first_down.wait_recv()

    below, here, above = hidden_row(0, r_up)
    s_up[...] = above.astype(BF16)
    acc2[0] = acc2[0] + here
    acc2[1] = acc2[1] + below

    @pl.when(has_up)
    def _():
        second_up.start()

    def final_row(r, received):
        out = jnp.maximum(acc2[r] + received[...].astype(F32) + b2, 0.0).astype(BF16)
        for g in range(groups):
            cols = min(GROUP, width - g * GROUP) * c2
            at = g * GROUP * c2
            o_ref[r, :, at : at + cols] = out[g * frames : (g + 1) * frames, 0:cols]

    @pl.when(has_up)
    def _():
        second_down.wait_recv()

    final_row(0, t_up)

    @pl.when(has_down)
    def _():
        second_up.wait_recv()

    final_row(1, t_down)

    @pl.when(has_next)
    def _():
        for one in halo_copies:
            one.wait_send()

    @pl.when(has_up)
    def _():
        first_up.wait_send()
        second_up.wait_send()

    @pl.when(has_down)
    def _():
        first_down.wait_send()
        second_down.wait_send()


def body(
    n_row,
    n_tm,
    features,
    frame_mask,
    norm_gain,
    input_weight,
    output_weight,
    first_kernel,
    first_bias,
    second_kernel,
    second_bias,
):
    frames, rows, width, channels = features.shape
    assert frames == WIN and rows == 2
    places = rows * width
    tokens = width * frames
    c1 = first_kernel.shape[2]
    c2 = second_kernel.shape[2]
    groups = (width + GROUP - 1) // GROUP
    x = features.transpose(1, 2, 0, 3).reshape(places * frames, channels)
    mask = jnp.broadcast_to(frame_mask.astype(F32)[:, None], (frames, 128))
    step = 2 * (places // 8)
    bounds = tuple(places - i * step for i in (4, 3, 2, 1, 0))
    bounds = (0,) + bounds[1:]
    slots = len(bounds) + 4
    vmem = pltpu.VMEM
    out = pl.pallas_call(
        functools.partial(kernel, width, bounds, n_row, n_tm),
        out_shape=jax.ShapeDtypeStruct((rows, frames, width * c2), BF16),
        in_specs=[pl.BlockSpec(memory_space=pltpu.VMEM)] * 9,
        out_specs=pl.BlockSpec(memory_space=pltpu.VMEM),
        scratch_shapes=[
            vmem((places * frames, channels), BF16),
            vmem((frames, 128), F32),
            vmem((places * frames, 3 * channels), BF16),
            vmem((places * frames, 2 * channels), BF16),
            vmem((places * frames, channels), BF16),
            vmem((HEADS * frames, channels), BF16),
            vmem((frames, HEADS * frames), F32),
            vmem((rows, tokens + 2 * frames, channels), BF16),
            vmem((TAPS * channels, TAPS * c1), BF16),
            vmem((TAPS * GROUP * c2, (GROUP + TAPS - 1) * c1), BF16),
            vmem((rows, tokens, c1), F32),
            vmem((tokens, c1), BF16),
            vmem((tokens, c1), BF16),
            vmem((tokens, c1), BF16),
            vmem((tokens, c1), BF16),
            vmem((rows, frames, (groups * GROUP + TAPS - 1) * c1), BF16),
            vmem((rows, groups * frames, GROUP * c2), F32),
            vmem((groups * frames, GROUP * c2), BF16),
            vmem((groups * frames, GROUP * c2), BF16),
            vmem((groups * frames, GROUP * c2), BF16),
            vmem((groups * frames, GROUP * c2), BF16),
            pltpu.SemaphoreType.DMA((slots,)),
            pltpu.SemaphoreType.DMA((slots,)),
        ],
        compiler_params=pltpu.CompilerParams(
            collective_id=0, has_side_effects=True, vmem_limit_bytes=60 * 1024 * 1024
        ),
    )(
        x,
        mask,
        norm_gain[None],
        input_weight,
        output_weight,
        first_kernel,
        first_bias[None],
        second_kernel.transpose(0, 2, 1),
        second_bias[None],
    )
    return out.transpose(1, 0, 2)


def solution(mesh):
    placed = (P("row", "tm", None, None), P("row"), P(), P(), P(), P(), P(), P(), P())
    return jax.shard_map(
        functools.partial(body, mesh.shape["row"], mesh.shape["tm"]),
        mesh=mesh,
        in_specs=placed,
        out_specs=P("row", "tm", None),
        check_vma=False,
    )
```

```python
import functools
import math

import jax
import jax.numpy as jnp
from jax import lax
from jax.experimental import pallas as pl
from jax.experimental.pallas import tpu as pltpu
from jax.sharding import PartitionSpec as P

HEADS = 8
WIN = 32
TAPS = 3
GROUP = 4
UNROLL = 4
CHUNKS = 4
NEG = -1e30
epsilon = 1e-05
MESH = pl.DeviceIdType.MESH
F32 = jnp.float32
BF16 = jnp.bfloat16


def layer_norm(field, gain):
    widened = field.astype(F32)
    average = jnp.mean(widened, axis=-1, keepdims=True)
    centered = widened - average
    variance = jnp.mean(centered * centered, axis=-1, keepdims=True)
    return (centered * lax.rsqrt(variance + epsilon) * gain).astype(BF16)


def dot(a, b):
    return jnp.dot(a, b, preferred_element_type=F32)


def dot_t(a, b):
    return lax.dot_general(a, b, (((1,), (1,)), ((), ())), preferred_element_type=F32)


def dot_tt(a, b):
    return lax.dot_general(a, b, (((0,), (0,)), ((), ())), preferred_element_type=F32)


def kernel(
    width,
    bounds,
    n_row,
    n_tm,
    x_ref,
    mask_ref,
    gain_ref,
    win_ref,
    wout_ref,
    k1_ref,
    b1_ref,
    k2_ref,
    b2_ref,
    o_ref,
    nrm,
    halo,
    pmask,
    qkv,
    hkv,
    att,
    headmask,
    bias,
    grid_x,
    w1,
    w2,
    acc,
    p_up,
    p_down,
    r_up,
    r_down,
    hid,
    acc2,
    s_up,
    s_down,
    t_up,
    t_down,
    send_sem,
    recv_sem,
):
    frames = WIN
    both = 2 * frames
    channels = x_ref.shape[1]
    head_size = channels // HEADS
    half = HEADS // 2
    c1 = k1_ref.shape[2]
    c2 = k2_ref.shape[1]
    row = lax.axis_index("row")
    tm = lax.axis_index("tm")
    has_prev, has_next = row > 0, row < n_row - 1
    has_up, has_down = tm > 0, tm < n_tm - 1
    chunks = len(bounds) - 1
    groups = (width + GROUP - 1) // GROUP
    edges = (0,) + tuple(b - 1 for b in bounds[1:-1]) + (width,)
    packs = (0,) + tuple((e - 1) // GROUP for e in edges[1:-1]) + (groups,)

    barrier = pltpu.get_barrier_semaphore()
    sides = (
        (has_prev, {"row": row - 1}),
        (has_next, {"row": row + 1}),
        (has_up, {"tm": tm - 1}),
        (has_down, {"tm": tm + 1}),
    )
    for present, where in sides:

        @pl.when(present)
        def _(where=where):
            pl.semaphore_signal(barrier, inc=1, device_id=where, device_id_type=MESH)

    pl.semaphore_wait(barrier, sum(present.astype(jnp.int32) for present, _ in sides))

    def copy(src, dst, slot, where):
        return pltpu.make_async_remote_copy(
            src_ref=src,
            dst_ref=dst,
            send_sem=send_sem.at[slot],
            recv_sem=recv_sem.at[slot],
            device_id=where,
            device_id_type=MESH,
        )

    nxt, up, down = {"row": row + 1}, {"tm": tm - 1}, {"tm": tm + 1}
    mask_copy = copy(mask_ref, pmask, 5 * chunks, nxt)
    halo_copies, first_up, first_down, second_up, second_down = [], [], [], [], []
    for c in range(chunks):
        part = pl.ds(bounds[c] * both, (bounds[c + 1] - bounds[c]) * both)
        halo_copies.append(copy(nrm.at[part], halo.at[part], c, nxt))
        part = pl.ds(edges[c] * frames, (edges[c + 1] - edges[c]) * frames)
        first_up.append(copy(p_up.at[part], r_down.at[part], chunks + c, up))
        first_down.append(copy(p_down.at[part], r_up.at[part], 2 * chunks + c, down))
        part = pl.ds(packs[c] * frames, (packs[c + 1] - packs[c]) * frames)
        second_up.append(copy(s_up.at[part], t_down.at[part], 3 * chunks + c, up))
        second_down.append(copy(s_down.at[part], t_up.at[part], 4 * chunks + c, down))

    def start(present, one):
        @pl.when(present)
        def _():
            one.start()

    def received(present, one):
        @pl.when(present)
        def _():
            one.wait_recv()

    start(has_next, mask_copy)

    @pl.when(jnp.logical_not(has_prev))
    def _():
        halo[...] = jnp.zeros_like(halo)
        pmask[...] = jnp.zeros_like(pmask)

    @pl.when(jnp.logical_not(has_up))
    def _():
        r_up[...] = jnp.zeros_like(r_up)
        t_up[...] = jnp.zeros_like(t_up)

    @pl.when(jnp.logical_not(has_down))
    def _():
        r_down[...] = jnp.zeros_like(r_down)
        t_down[...] = jnp.zeros_like(t_down)

    gain = gain_ref[...]
    for c in range(chunks):
        part = slice(bounds[c] * both, bounds[c + 1] * both)
        normed = layer_norm(x_ref[part], gain)
        nrm[part] = normed
        qkv[part] = dot(normed, win_ref[...]).astype(BF16)
        start(has_next, halo_copies[c])

    for tap in range(TAPS * TAPS):
        a, b = tap // TAPS, tap % TAPS
        w1[b * channels : (b + 1) * channels, a * c1 : (a + 1) * c1] = k1_ref[tap]
    w2[...] = jnp.zeros_like(w2)
    for a in range(TAPS):
        for o in range(GROUP):
            for b in range(TAPS):
                r0 = (a * GROUP + o) * c2
                w2[r0 : r0 + c2, (o + b) * c1 : (o + b + 1) * c1] = k2_ref[a * TAPS + b]
    end = width * both
    grid_x[0:both] = jnp.zeros((both, channels), BF16)
    grid_x[end + both : end + 2 * both] = jnp.zeros((both, channels), BF16)
    if qkv.shape[0] > end:
        qkv[end:] = jnp.zeros_like(qkv[end:])
        hkv[end:] = jnp.zeros_like(hkv[end:])
    for r in range(2):
        hid[r, :, 0:c1] = jnp.zeros((frames, c1), BF16)
        tail = hid.shape[2] - (width + 1) * c1
        hid[r, :, (width + 1) * c1 :] = jnp.zeros((frames, tail), BF16)

    lane = lax.broadcasted_iota(jnp.int32, (HEADS * frames, channels), 1)
    sub = lax.broadcasted_iota(jnp.int32, (HEADS * frames, channels), 0)
    headmask[...] = (lane // head_size == sub // frames).astype(F32).astype(BF16)

    scale = 1.0 / math.sqrt(head_size)
    slot_s = lax.broadcasted_iota(jnp.int32, (frames, HEADS * frames), 0)
    slot_t = lax.broadcasted_iota(jnp.int32, (frames, HEADS * frames), 1) % frames
    own = slot_s <= slot_t

    received(has_prev, mask_copy)
    eye_s = lax.broadcasted_iota(jnp.int32, (frames, frames), 0)
    eye_t = lax.broadcasted_iota(jnp.int32, (frames, frames), 1)

    def column(ref):
        spread = jnp.broadcast_to(ref[...].astype(F32), (frames, frames))
        picked = jnp.sum(jnp.where(eye_s == eye_t, spread, 0.0), axis=1, keepdims=True)
        return jnp.broadcast_to(picked, (frames, HEADS * frames))

    seen = jnp.where(own, jnp.where(slot_s == slot_t, 1.0, column(mask_ref)), column(pmask))
    bias[...] = jnp.where(seen == 1.0, 0.0, NEG)

    lane_head = lax.broadcasted_iota(jnp.int32, (frames, channels // 2), 1) // head_size

    def scores(p):
        rows = pl.ds(pl.multiple_of(p * frames, frames), frames)
        q = qkv[rows, 0:channels]
        k = jnp.concatenate([hkv[rows, 0:channels], qkv[rows, channels : 2 * channels]], axis=0)
        spread = jnp.concatenate([q] * HEADS, axis=0) * headmask[...]
        return dot_t(k, spread)

    def soften(s):
        s = jnp.where(own, s[frames:], s[:frames]) + bias[...]
        peak = jnp.max(s, axis=0, keepdims=True)
        powers = jnp.exp((s - peak) * scale)
        w = powers * (1.0 / jnp.sum(powers, axis=0, keepdims=True))
        return jnp.concatenate([jnp.where(own, 0.0, w), jnp.where(own, w, 0.0)], axis=0).astype(BF16)

    def gather(p, w):
        rows = pl.ds(pl.multiple_of(p * frames, frames), frames)
        v = jnp.concatenate(
            [hkv[rows, channels : 2 * channels], qkv[rows, 2 * channels : 3 * channels]], axis=0
        )
        outs = []
        for g in range(2):
            cols = slice(g * channels // 2, (g + 1) * channels // 2)
            r = dot_tt(w[:, g * half * frames : (g + 1) * half * frames], v[:, cols])
            total_g = r[0:frames]
            for h in range(1, half):
                total_g = jnp.where(lane_head == h, r[h * frames : (h + 1) * frames], total_g)
            outs.append(total_g)
        att[rows] = jnp.concatenate(outs, axis=1).astype(BF16)

    def step(i, carry):
        ids = [UNROLL * i + u for u in range(UNROLL)]
        raw = [scores(p) for p in ids]
        soft = [soften(s) for s in raw]
        for p, w in zip(ids, soft):
            gather(p, w)
        return carry

    b2 = jnp.concatenate([b2_ref[...]] * GROUP, axis=1)
    span = (GROUP + TAPS - 1) * c1

    def split(full, n):
        return full[:, 0:n], full[:, n : 2 * n], full[:, 2 * n : 3 * n]

    def convolve_first(c):
        lo, hi = edges[c], edges[c + 1]
        window = jnp.concatenate(
            [grid_x[(lo + b) * both : (hi + b) * both] for b in range(TAPS)], axis=1
        )
        below, here, above = split(dot(window, w1[...]), c1)
        for col in range(lo, hi):
            a = slice((col - lo) * both, (col - lo) * both + frames)
            b = slice((col - lo) * both + frames, (col - lo + 1) * both)
            rows = slice(col * frames, (col + 1) * frames)
            p_up[rows] = above[a].astype(BF16)
            p_down[rows] = below[b].astype(BF16)
            acc[0, rows] = here[a] + above[b]
            acc[1, rows] = here[b] + below[a]
        start(has_up, first_up[c])
        start(has_down, first_down[c])

    def convolve_second(c):
        received(has_down, first_up[c])
        received(has_up, first_down[c])
        for r, came in ((0, r_up), (1, r_down)):
            for col in range(edges[c], edges[c + 1]):
                rows = slice(col * frames, (col + 1) * frames)
                h = jnp.maximum(acc[r, rows] + came[rows].astype(F32) + b1_ref[...], 0.0)
                hid[r, :, (col + 1) * c1 : (col + 2) * c1] = h.astype(BF16)
        lo, hi = packs[c], packs[c + 1]
        window = jnp.concatenate(
            [
                hid[r, :, g * GROUP * c1 : g * GROUP * c1 + span]
                for r in range(2)
                for g in range(lo, hi)
            ],
            axis=0,
        )
        below, here, above = split(dot_t(window, w2[...]), GROUP * c2)
        n = (hi - lo) * frames
        rows = slice(lo * frames, hi * frames)
        s_up[rows] = above[:n].astype(BF16)
        s_down[rows] = below[n:].astype(BF16)
        acc2[0, rows] = here[:n] + above[n:]
        acc2[1, rows] = here[n:] + below[:n]
        start(has_up, second_up[c])
        start(has_down, second_down[c])

    def final(c):
        received(has_down, second_up[c])
        received(has_up, second_down[c])
        for r, came in ((0, t_up), (1, t_down)):
            for g in range(packs[c], packs[c + 1]):
                rows = slice(g * frames, (g + 1) * frames)
                out = jnp.maximum(acc2[r, rows] + came[rows].astype(F32) + b2, 0.0).astype(BF16)
                cols = min(GROUP, width - g * GROUP) * c2
                at = g * GROUP * c2
                o_ref[r, :, at : at + cols] = out[:, 0:cols]

    for c in range(chunks):
        received(has_prev, halo_copies[c])
        part = slice(bounds[c] * both, bounds[c + 1] * both)
        hkv[part] = dot(halo[part], win_ref[:, channels : 3 * channels]).astype(BF16)
        last = -(-bounds[c + 1] * 2 // UNROLL)
        lax.fori_loop(bounds[c] * 2 // UNROLL, last, step, 0)
        mixed = x_ref[part].astype(F32) + dot(att[part], wout_ref[...])
        grid_x[(bounds[c] + 1) * both : (bounds[c + 1] + 1) * both] = mixed.astype(BF16)
        convolve_first(c)
        if c > 0:
            convolve_second(c - 1)
    for c in range(chunks - 1):
        final(c)
    convolve_second(chunks - 1)
    final(chunks - 1)

    @pl.when(has_next)
    def _():
        for one in [mask_copy] + halo_copies:
            one.wait_send()

    @pl.when(has_up)
    def _():
        for one in first_up + second_up:
            one.wait_send()

    @pl.when(has_down)
    def _():
        for one in first_down + second_down:
            one.wait_send()


def body(
    n_row,
    n_tm,
    features,
    frame_mask,
    norm_gain,
    input_weight,
    output_weight,
    first_kernel,
    first_bias,
    second_kernel,
    second_bias,
):
    frames, rows, width, channels = features.shape
    assert frames == WIN and rows == 2
    places = rows * width
    tokens = places * frames
    padded = -(-places // UNROLL) * UNROLL * frames
    c1 = first_kernel.shape[2]
    c2 = second_kernel.shape[2]
    groups = (width + GROUP - 1) // GROUP
    x = features.transpose(2, 1, 0, 3).reshape(tokens, channels)
    even = UNROLL // 2
    piece = even * -(-width // (even * CHUNKS))
    bounds = tuple(range(0, width, piece)) + (width,)
    slots = 5 * (len(bounds) - 1) + 1
    vmem = pltpu.VMEM
    out = pl.pallas_call(
        functools.partial(kernel, width, bounds, n_row, n_tm),
        out_shape=jax.ShapeDtypeStruct((rows, frames, width * c2), BF16),
        in_specs=[pl.BlockSpec(memory_space=pltpu.VMEM)] * 9,
        out_specs=pl.BlockSpec(memory_space=pltpu.VMEM),
        scratch_shapes=[
            vmem((tokens, channels), BF16),
            vmem((tokens, channels), BF16),
            vmem((1, frames), jnp.int32),
            vmem((padded, 3 * channels), BF16),
            vmem((padded, 2 * channels), BF16),
            vmem((padded, channels), BF16),
            vmem((HEADS * frames, channels), BF16),
            vmem((frames, HEADS * frames), F32),
            vmem(((width + 2) * rows * frames, channels), BF16),
            vmem((TAPS * channels, TAPS * c1), BF16),
            vmem((TAPS * GROUP * c2, (GROUP + TAPS - 1) * c1), BF16),
            vmem((rows, width * frames, c1), F32),
            vmem((width * frames, c1), BF16),
            vmem((width * frames, c1), BF16),
            vmem((width * frames, c1), BF16),
            vmem((width * frames, c1), BF16),
            vmem((rows, frames, (groups * GROUP + TAPS - 1) * c1), BF16),
            vmem((rows, groups * frames, GROUP * c2), F32),
            vmem((groups * frames, GROUP * c2), BF16),
            vmem((groups * frames, GROUP * c2), BF16),
            vmem((groups * frames, GROUP * c2), BF16),
            vmem((groups * frames, GROUP * c2), BF16),
            pltpu.SemaphoreType.DMA((slots,)),
            pltpu.SemaphoreType.DMA((slots,)),
        ],
        compiler_params=pltpu.CompilerParams(
            collective_id=0, has_side_effects=True, vmem_limit_bytes=30 * 1024 * 1024
        ),
    )(
        x,
        frame_mask[None],
        norm_gain[None],
        input_weight,
        output_weight,
        first_kernel,
        first_bias[None],
        second_kernel.transpose(0, 2, 1),
        second_bias[None],
    )
    return out.transpose(1, 0, 2)


def solution(mesh):
    placed = (P("row", "tm", None, None), P("row"), P(), P(), P(), P(), P(), P(), P())
    return jax.shard_map(
        functools.partial(body, mesh.shape["row"], mesh.shape["tm"]),
        mesh=mesh,
        in_specs=placed,
        out_specs=P("row", "tm", None),
        check_vma=False,
    )
```

```python
import functools
import math

import jax
import jax.numpy as jnp
from jax import lax
from jax.experimental import pallas as pl
from jax.experimental.pallas import tpu as pltpu
from jax.sharding import PartitionSpec as P

HEADS = 8
WIN = 32
TAPS = 3
GROUP = 4
UNROLL = 4
CUTS = (0.22, 0.48, 0.76, 0.92)
NEG = -1e30
epsilon = 1e-05
MESH = pl.DeviceIdType.MESH
F32 = jnp.float32
BF16 = jnp.bfloat16


def layer_norm(field, gain):
    widened = field.astype(F32)
    average = jnp.mean(widened, axis=-1, keepdims=True)
    centered = widened - average
    variance = jnp.mean(centered * centered, axis=-1, keepdims=True)
    return (centered * lax.rsqrt(variance + epsilon) * gain).astype(BF16)


def dot(a, b):
    return jnp.dot(a, b, preferred_element_type=F32)


def dot_t(a, b):
    return lax.dot_general(a, b, (((1,), (1,)), ((), ())), preferred_element_type=F32)


def dot_tt(a, b):
    return lax.dot_general(a, b, (((0,), (0,)), ((), ())), preferred_element_type=F32)


def kernel(
    width,
    bounds,
    n_row,
    n_tm,
    x_ref,
    mask_ref,
    gain_ref,
    win_ref,
    wout_ref,
    k1_ref,
    b1_ref,
    k2_ref,
    b2_ref,
    o_ref,
    nrm,
    halo,
    pmask,
    qkv,
    hkv,
    att,
    headmask,
    bias,
    grid_x,
    w1,
    w2,
    acc,
    p_up,
    p_down,
    r_up,
    r_down,
    hid,
    acc2,
    s_up,
    s_down,
    t_up,
    t_down,
    send_sem,
    recv_sem,
):
    frames = WIN
    both = 2 * frames
    channels = x_ref.shape[1]
    head_size = channels // HEADS
    half = HEADS // 2
    c1 = k1_ref.shape[2]
    c2 = k2_ref.shape[1]
    row = lax.axis_index("row")
    tm = lax.axis_index("tm")
    has_prev, has_next = row > 0, row < n_row - 1
    has_up, has_down = tm > 0, tm < n_tm - 1
    chunks = len(bounds) - 1
    groups = (width + GROUP - 1) // GROUP
    edges = (0,) + tuple(b - 1 for b in bounds[1:-1]) + (width,)
    packs = (0,) + tuple((e - 1) // GROUP for e in edges[1:-1]) + (groups,)

    barrier = pltpu.get_barrier_semaphore()
    sides = (
        (has_prev, {"row": row - 1}),
        (has_next, {"row": row + 1}),
        (has_up, {"tm": tm - 1}),
        (has_down, {"tm": tm + 1}),
    )
    for present, where in sides:

        @pl.when(present)
        def _(where=where):
            pl.semaphore_signal(barrier, inc=1, device_id=where, device_id_type=MESH)

    pl.semaphore_wait(barrier, sum(present.astype(jnp.int32) for present, _ in sides))

    def copy(src, dst, slot, where):
        return pltpu.make_async_remote_copy(
            src_ref=src,
            dst_ref=dst,
            send_sem=send_sem.at[slot],
            recv_sem=recv_sem.at[slot],
            device_id=where,
            device_id_type=MESH,
        )

    nxt, up, down = {"row": row + 1}, {"tm": tm - 1}, {"tm": tm + 1}
    mask_copy = copy(mask_ref, pmask, 5 * chunks, nxt)
    halo_copies, first_up, first_down, second_up, second_down = [], [], [], [], []
    for c in range(chunks):
        part = pl.ds(bounds[c] * both, (bounds[c + 1] - bounds[c]) * both)
        halo_copies.append(copy(nrm.at[part], halo.at[part], c, nxt))
        part = pl.ds(edges[c] * frames, (edges[c + 1] - edges[c]) * frames)
        first_up.append(copy(p_up.at[part], r_down.at[part], chunks + c, up))
        first_down.append(copy(p_down.at[part], r_up.at[part], 2 * chunks + c, down))
        part = pl.ds(packs[c] * frames, (packs[c + 1] - packs[c]) * frames)
        second_up.append(copy(s_up.at[part], t_down.at[part], 3 * chunks + c, up))
        second_down.append(copy(s_down.at[part], t_up.at[part], 4 * chunks + c, down))

    def start(present, one):
        @pl.when(present)
        def _():
            one.start()

    def received(present, one):
        @pl.when(present)
        def _():
            one.wait_recv()

    start(has_next, mask_copy)

    @pl.when(jnp.logical_not(has_prev))
    def _():
        halo[...] = jnp.zeros_like(halo)
        pmask[...] = jnp.zeros_like(pmask)

    @pl.when(jnp.logical_not(has_up))
    def _():
        r_up[...] = jnp.zeros_like(r_up)
        t_up[...] = jnp.zeros_like(t_up)

    @pl.when(jnp.logical_not(has_down))
    def _():
        r_down[...] = jnp.zeros_like(r_down)
        t_down[...] = jnp.zeros_like(t_down)

    gain = gain_ref[...]
    for c in range(chunks):
        part = slice(bounds[c] * both, bounds[c + 1] * both)
        normed = layer_norm(x_ref[part], gain)
        nrm[part] = normed
        qkv[part] = dot(normed, win_ref[...]).astype(BF16)
        start(has_next, halo_copies[c])

    for tap in range(TAPS * TAPS):
        a, b = tap // TAPS, tap % TAPS
        w1[b * channels : (b + 1) * channels, a * c1 : (a + 1) * c1] = k1_ref[tap]
    w2[...] = jnp.zeros_like(w2)
    for a in range(TAPS):
        for o in range(GROUP):
            for b in range(TAPS):
                r0 = (a * GROUP + o) * c2
                w2[r0 : r0 + c2, (o + b) * c1 : (o + b + 1) * c1] = k2_ref[a * TAPS + b]
    end = width * both
    grid_x[0:both] = jnp.zeros((both, channels), BF16)
    grid_x[end + both : end + 2 * both] = jnp.zeros((both, channels), BF16)
    if qkv.shape[0] > end:
        qkv[end:] = jnp.zeros_like(qkv[end:])
        hkv[end:] = jnp.zeros_like(hkv[end:])
    for r in range(2):
        hid[r, :, 0:c1] = jnp.zeros((frames, c1), BF16)
        tail = hid.shape[2] - (width + 1) * c1
        hid[r, :, (width + 1) * c1 :] = jnp.zeros((frames, tail), BF16)

    lane = lax.broadcasted_iota(jnp.int32, (HEADS * frames, channels), 1)
    sub = lax.broadcasted_iota(jnp.int32, (HEADS * frames, channels), 0)
    headmask[...] = (lane // head_size == sub // frames).astype(F32).astype(BF16)

    scale = 1.0 / math.sqrt(head_size)
    slot_s = lax.broadcasted_iota(jnp.int32, (frames, HEADS * frames), 0)
    slot_t = lax.broadcasted_iota(jnp.int32, (frames, HEADS * frames), 1) % frames
    own = slot_s <= slot_t

    received(has_prev, mask_copy)
    eye_s = lax.broadcasted_iota(jnp.int32, (frames, frames), 0)
    eye_t = lax.broadcasted_iota(jnp.int32, (frames, frames), 1)

    def column(ref):
        spread = jnp.broadcast_to(ref[...].astype(F32), (frames, frames))
        picked = jnp.sum(jnp.where(eye_s == eye_t, spread, 0.0), axis=1, keepdims=True)
        return jnp.broadcast_to(picked, (frames, HEADS * frames))

    seen = jnp.where(own, jnp.where(slot_s == slot_t, 1.0, column(mask_ref)), column(pmask))
    bias[...] = jnp.where(seen == 1.0, 0.0, NEG)

    lane_head = lax.broadcasted_iota(jnp.int32, (frames, channels // 2), 1) // head_size

    def scores(p):
        rows = pl.ds(pl.multiple_of(p * frames, frames), frames)
        q = qkv[rows, 0:channels]
        k = jnp.concatenate([hkv[rows, 0:channels], qkv[rows, channels : 2 * channels]], axis=0)
        spread = jnp.concatenate([q] * HEADS, axis=0) * headmask[...]
        return dot_t(k, spread)

    def soften(s):
        s = jnp.where(own, s[frames:], s[:frames]) + bias[...]
        peak = jnp.max(s, axis=0, keepdims=True)
        powers = jnp.exp((s - peak) * scale)
        w = powers * (1.0 / jnp.sum(powers, axis=0, keepdims=True))
        return jnp.concatenate([jnp.where(own, 0.0, w), jnp.where(own, w, 0.0)], axis=0).astype(BF16)

    def gather(p, w):
        rows = pl.ds(pl.multiple_of(p * frames, frames), frames)
        v = jnp.concatenate(
            [hkv[rows, channels : 2 * channels], qkv[rows, 2 * channels : 3 * channels]], axis=0
        )
        outs = []
        for g in range(2):
            cols = slice(g * channels // 2, (g + 1) * channels // 2)
            r = dot_tt(w[:, g * half * frames : (g + 1) * half * frames], v[:, cols])
            total_g = r[0:frames]
            for h in range(1, half):
                total_g = jnp.where(lane_head == h, r[h * frames : (h + 1) * frames], total_g)
            outs.append(total_g)
        att[rows] = jnp.concatenate(outs, axis=1).astype(BF16)

    def step(i, carry):
        ids = [UNROLL * i + u for u in range(UNROLL)]
        raw = [scores(p) for p in ids]
        soft = [soften(s) for s in raw]
        for p, w in zip(ids, soft):
            gather(p, w)
        return carry

    b2 = jnp.concatenate([b2_ref[...]] * GROUP, axis=1)
    span = (GROUP + TAPS - 1) * c1

    def split(full, n):
        return full[:, 0:n], full[:, n : 2 * n], full[:, 2 * n : 3 * n]

    def convolve_first(c):
        lo, hi = edges[c], edges[c + 1]
        window = jnp.concatenate(
            [grid_x[(lo + b) * both : (hi + b) * both] for b in range(TAPS)], axis=1
        )
        below, here, above = split(dot(window, w1[...]), c1)
        for col in range(lo, hi):
            a = slice((col - lo) * both, (col - lo) * both + frames)
            b = slice((col - lo) * both + frames, (col - lo + 1) * both)
            rows = slice(col * frames, (col + 1) * frames)
            p_up[rows] = above[a].astype(BF16)
            p_down[rows] = below[b].astype(BF16)
            acc[0, rows] = here[a] + above[b]
            acc[1, rows] = here[b] + below[a]
        start(has_up, first_up[c])
        start(has_down, first_down[c])

    def convolve_second(c):
        received(has_down, first_up[c])
        received(has_up, first_down[c])
        for r, came in ((0, r_up), (1, r_down)):
            for col in range(edges[c], edges[c + 1]):
                rows = slice(col * frames, (col + 1) * frames)
                h = jnp.maximum(acc[r, rows] + came[rows].astype(F32) + b1_ref[...], 0.0)
                hid[r, :, (col + 1) * c1 : (col + 2) * c1] = h.astype(BF16)
        lo, hi = packs[c], packs[c + 1]
        window = jnp.concatenate(
            [
                hid[r, :, g * GROUP * c1 : g * GROUP * c1 + span]
                for r in range(2)
                for g in range(lo, hi)
            ],
            axis=0,
        )
        below, here, above = split(dot_t(window, w2[...]), GROUP * c2)
        n = (hi - lo) * frames
        rows = slice(lo * frames, hi * frames)
        s_up[rows] = above[:n].astype(BF16)
        s_down[rows] = below[n:].astype(BF16)
        acc2[0, rows] = here[:n] + above[n:]
        acc2[1, rows] = here[n:] + below[:n]
        start(has_up, second_up[c])
        start(has_down, second_down[c])

    def final(c):
        received(has_down, second_up[c])
        received(has_up, second_down[c])
        for r, came in ((0, t_up), (1, t_down)):
            for g in range(packs[c], packs[c + 1]):
                rows = slice(g * frames, (g + 1) * frames)
                out = jnp.maximum(acc2[r, rows] + came[rows].astype(F32) + b2, 0.0).astype(BF16)
                cols = min(GROUP, width - g * GROUP) * c2
                at = g * GROUP * c2
                o_ref[r, :, at : at + cols] = out[:, 0:cols]

    for c in range(chunks):
        received(has_prev, halo_copies[c])
        part = slice(bounds[c] * both, bounds[c + 1] * both)
        hkv[part] = dot(halo[part], win_ref[:, channels : 3 * channels]).astype(BF16)
        last = -(-bounds[c + 1] * 2 // UNROLL)
        lax.fori_loop(bounds[c] * 2 // UNROLL, last, step, 0)
        mixed = x_ref[part].astype(F32) + dot(att[part], wout_ref[...])
        grid_x[(bounds[c] + 1) * both : (bounds[c + 1] + 1) * both] = mixed.astype(BF16)
        convolve_first(c)
        if c >= 2:
            convolve_second(c - 2)
    for c in range(chunks - 2, chunks):
        convolve_second(c)
    for c in range(chunks):
        final(c)

    @pl.when(has_next)
    def _():
        for one in [mask_copy] + halo_copies:
            one.wait_send()

    @pl.when(has_up)
    def _():
        for one in first_up + second_up:
            one.wait_send()

    @pl.when(has_down)
    def _():
        for one in first_down + second_down:
            one.wait_send()


def body(
    n_row,
    n_tm,
    features,
    frame_mask,
    norm_gain,
    input_weight,
    output_weight,
    first_kernel,
    first_bias,
    second_kernel,
    second_bias,
):
    frames, rows, width, channels = features.shape
    assert frames == WIN and rows == 2
    places = rows * width
    tokens = places * frames
    padded = -(-places // UNROLL) * UNROLL * frames
    c1 = first_kernel.shape[2]
    c2 = second_kernel.shape[2]
    groups = (width + GROUP - 1) // GROUP
    x = features.transpose(2, 1, 0, 3).reshape(tokens, channels)
    even = UNROLL // 2
    bounds = (0,) + tuple(even * round(width * cut / even) for cut in CUTS) + (width,)
    slots = 5 * (len(bounds) - 1) + 1
    vmem = pltpu.VMEM
    out = pl.pallas_call(
        functools.partial(kernel, width, bounds, n_row, n_tm),
        out_shape=jax.ShapeDtypeStruct((rows, frames, width * c2), BF16),
        in_specs=[pl.BlockSpec(memory_space=pltpu.VMEM)] * 9,
        out_specs=pl.BlockSpec(memory_space=pltpu.VMEM),
        scratch_shapes=[
            vmem((tokens, channels), BF16),
            vmem((tokens, channels), BF16),
            vmem((1, frames), jnp.int32),
            vmem((padded, 3 * channels), BF16),
            vmem((padded, 2 * channels), BF16),
            vmem((padded, channels), BF16),
            vmem((HEADS * frames, channels), BF16),
            vmem((frames, HEADS * frames), F32),
            vmem(((width + 2) * rows * frames, channels), BF16),
            vmem((TAPS * channels, TAPS * c1), BF16),
            vmem((TAPS * GROUP * c2, (GROUP + TAPS - 1) * c1), BF16),
            vmem((rows, width * frames, c1), F32),
            vmem((width * frames, c1), BF16),
            vmem((width * frames, c1), BF16),
            vmem((width * frames, c1), BF16),
            vmem((width * frames, c1), BF16),
            vmem((rows, frames, (groups * GROUP + TAPS - 1) * c1), BF16),
            vmem((rows, groups * frames, GROUP * c2), F32),
            vmem((groups * frames, GROUP * c2), BF16),
            vmem((groups * frames, GROUP * c2), BF16),
            vmem((groups * frames, GROUP * c2), BF16),
            vmem((groups * frames, GROUP * c2), BF16),
            pltpu.SemaphoreType.DMA((slots,)),
            pltpu.SemaphoreType.DMA((slots,)),
        ],
        compiler_params=pltpu.CompilerParams(
            collective_id=0, has_side_effects=True, vmem_limit_bytes=30 * 1024 * 1024
        ),
    )(
        x,
        frame_mask[None],
        norm_gain[None],
        input_weight,
        output_weight,
        first_kernel,
        first_bias[None],
        second_kernel.transpose(0, 2, 1),
        second_bias[None],
    )
    return out.transpose(1, 0, 2)


def solution(mesh):
    placed = (P("row", "tm", None, None), P("row"), P(), P(), P(), P(), P(), P(), P())
    return jax.shard_map(
        functools.partial(body, mesh.shape["row"], mesh.shape["tm"]),
        mesh=mesh,
        in_specs=placed,
        out_specs=P("row", "tm", None),
        check_vma=False,
    )
```
